32 devices in a mesh: hus: 16 (over z, x, core), wif: 2 (over y).
Axes of the slice: x: 2, y: 2, z: 4, core: 2. Of those that a mesh axis runs over, the one named last changes fastest.
Arguments:
- husband_codes: int32 [4096, 192], P(('hus', 'wif')), may hold values from -127 to 127
- husband_scales: float32 [128, 192], P(('hus', 'wif')), may hold values from 0.002 to 0.02
- wife_codes: int32 [16384, 192], P(('wif', 'hus')), may hold values from -127 to 127
- wife_scales: float32 [512, 192], P(('wif', 'hus')), may hold values from 0.002 to 0.02
- affinity: bfloat16 [192, 192], replicated, may hold values from -0.119628906 to 0.119628906
- husband_mass: float32 [4096], P('hus'), may hold values from 0.5 to 4.5, as said below
- wife_mass: float32 [16384], replicated, may hold values from 0.5 to 2
Outputs:
- row_potential: float32 [4096], P('hus')
- col_potential: float32 [16384], P('wif')
- moments: float32 [36864], P(('hus', 'wif'))
The draws below stay inside these ranges and needn't reach their ends.
Inputs may be any that keep to these rules, and one draw needn't show every extreme that they name: `husband_mass`: every mass is positive.
All inputs are finite; a program needn't handle non-finite values.
Results may differ from the reference program's by a relative error of at most 0.0023.
Values may be sent and summed in bfloat16 or wider, within the bound.
No kernel may reach another device: no remote copies, remote signals or barrier semaphores. Data moves between devices by JAX's collectives and lax.ppermute only.
A program may use at most 64 MiB of HBM per device.

```python
import math
import jax
import jax.numpy as jnp
from jax import lax

TRAITS = 192
GROUP = 32
SWEEPS = 2
NH = 4096
NW = 16384


def draw_husband_mass(key, part):
    base = jax.random.uniform(key, (NH,), jnp.float32, 0.5, 1.5)
    position = jnp.arange(NH, dtype=jnp.float32) / NH
    return base * (1.0 + 2.0 * position)


def touch_ends(result, rng, least, top_value):
    index_at = [jax.random.randint(jax.random.fold_in(rng, axis), (), 0, length) for axis, length in enumerate(result.shape)]
    main_axis = result.shape.index(max(result.shape))
    next_to = index_at[:main_axis] + [(index_at[main_axis] + 1) % result.shape[main_axis]] + index_at[main_axis + 1:]
    return result.at[tuple(index_at)].set(least).at[tuple(next_to)].set(top_value)


def block_levels(own_key, dims, split, smallest, largest):
    def one(axis_at, shards_of):
        heights = jax.random.uniform(jax.random.fold_in(jax.random.fold_in(own_key, 6), axis_at), (shards_of,), jnp.float32, smallest / len(split), largest / len(split))
        return jnp.repeat(jnp.exp(heights), dims[axis_at] // shards_of).reshape((-1,) + (1,) * (len(dims) - axis_at - 1))

    factor_of = one(*split[0])
    for cut in split[1:]:
        factor_of = factor_of * one(*cut)
    return factor_of


def normal_values(rng, extent, spread, reach, held_as=jnp.bfloat16):
    return jnp.clip(spread * jax.random.normal(rng, extent, jnp.float32), -reach, reach).astype(held_as)


def setup_inputs(seed: int = 0) -> dict:
    keys = jax.random.split(jax.random.key(seed), 8)
    husband_codes = touch_ends(jax.random.randint(keys[0], (NH, TRAITS), -127, 128), jax.random.fold_in(keys[0], 1), -127, 127).astype(jnp.int32)
    husband_scales = jnp.clip(jnp.exp(math.log(0.02) - 2.30258502 * jax.random.uniform(keys[1], (NH // GROUP, TRAITS), jnp.float32) ** block_levels(keys[1], (NH // GROUP, TRAITS), ((0, 32),), -0.2, 0.2)), 0.002, 0.02)
    wife_codes = touch_ends(jax.random.randint(keys[2], (NW, TRAITS), -127, 128), jax.random.fold_in(keys[2], 1), -127, 127).astype(jnp.int32)
    wife_scales = jnp.clip(jnp.exp(math.log(0.02) - 2.30258502 * jax.random.uniform(keys[3], (NW // GROUP, TRAITS), jnp.float32) ** block_levels(keys[3], (NW // GROUP, TRAITS), ((0, 32),), -0.2, 0.2)), 0.002, 0.02)
    affinity = normal_values(keys[4], (TRAITS, TRAITS), 0.02, 0.119628906)
    husband_mass = draw_husband_mass(jax.random.fold_in(keys[7], 71), 0)
    wife_mass = jnp.clip(jnp.exp(jax.random.uniform(keys[6], (NW,), jnp.float32, math.log(0.5), math.log(2.0))), 0.5, 2.0)
    return {"husband_codes": husband_codes, "husband_scales": husband_scales, "wife_codes": wife_codes, "wife_scales": wife_scales, "affinity": affinity, "husband_mass": husband_mass, "wife_mass": wife_mass}


def dequantize(trait_codes, scale_table):
    row_count, trait_count = trait_codes.shape
    groups = scale_table.shape[0]
    values = trait_codes.reshape(groups, row_count // groups, trait_count).astype(jnp.float32) * scale_table[:, None, :]
    return values.reshape(row_count, trait_count).astype(jnp.bfloat16)


def kernel_block(left_rows, wives):
    scores = lax.dot_general(left_rows, wives, (((1,), (1,)), ((), ())), preferred_element_type=jnp.float32)
    return jnp.exp(scores).astype(jnp.bfloat16)


def reference(husband_codes, husband_scales, wife_codes, wife_scales, affinity, husband_mass, wife_mass):
    husbands = dequantize(husband_codes, husband_scales)
    wives = dequantize(wife_codes, wife_scales)
    left_proj = jnp.dot(husbands, affinity, preferred_element_type=jnp.float32).astype(jnp.bfloat16)
    count_h = husbands.shape[0]
    count_w = wives.shape[0]
    trait_count = husbands.shape[1]
    block_rows = min(256, count_h)
    nblocks = count_h // block_rows
    left_blocks = left_proj.reshape(nblocks, block_rows, trait_count)
    mass_blocks = husband_mass.reshape(nblocks, block_rows)
    column_pot = jnp.ones((count_w,), jnp.float32)
    row_pot = jnp.zeros((count_h,), jnp.float32)
    for sweep_index in range(SWEEPS):
        def sweep_step(carried, inputs):
            left_rows, masses = inputs
            kernel_tile = kernel_block(left_rows, wives).astype(jnp.float32)
            row_mean = jnp.dot(kernel_tile, column_pot, precision=lax.Precision.HIGHEST) / count_w
            potentials = masses / row_mean
            return carried + jnp.dot(potentials, kernel_tile, precision=lax.Precision.HIGHEST), potentials
        summed, potentials = lax.scan(sweep_step, jnp.zeros((count_w,), jnp.float32), (left_blocks, mass_blocks))
        row_pot = potentials.reshape(-1)
        column_pot = wife_mass / (summed / count_h)
    trait_blocks = husbands.reshape(nblocks, block_rows, trait_count)
    pot_blocks = row_pot.reshape(nblocks, block_rows)

    def moment_step(carried, inputs):
        left_rows, potentials, traits = inputs
        kernel_tile = kernel_block(left_rows, wives).astype(jnp.float32)
        plan = (potentials[:, None] * kernel_tile * column_pot[None, :]).astype(jnp.bfloat16)
        weighted = jnp.dot(plan, wives, preferred_element_type=jnp.float32)
        return carried + jnp.dot(traits.astype(jnp.float32).T, weighted, precision=lax.Precision.HIGHEST), None

    summed, unused = lax.scan(moment_step, jnp.zeros((trait_count, trait_count), jnp.float32), (left_blocks, pot_blocks, trait_blocks))
    moments = summed * (trait_count / (count_h * count_w))
    return row_pot, column_pot, moments.reshape(-1)
```

```python
import functools

import jax
import jax.numpy as jnp
from jax import lax
from jax.experimental import pallas as pl
from jax.experimental.pallas import tpu as pltpu
from jax.sharding import Mesh
from jax.sharding import PartitionSpec as P

SWEEPS = 2
AXES = ("hh", "core", "wif")
CHIPS = ("hh", "wif")
F32 = jnp.float32
BF16 = jnp.bfloat16
VMEM = pl.BlockSpec(memory_space=pltpu.VMEM)


def call(kernel, outs, *args, scratch=(), flops=0, limit=24 << 20, name=None):
    size = sum(a.size * a.dtype.itemsize for a in args)
    size += sum(o.size * o.dtype.itemsize for o in outs)
    return pl.pallas_call(
        kernel,
        out_shape=outs,
        in_specs=[VMEM] * len(args),
        out_specs=[VMEM] * len(outs),
        scratch_shapes=scratch,
        compiler_params=pltpu.CompilerParams(vmem_limit_bytes=limit),
        cost_estimate=pl.CostEstimate(flops=flops, bytes_accessed=size, transcendentals=0),
        name=name,
    )(*args)


def shape(dims, dtype=F32):
    return jax.ShapeDtypeStruct(dims, dtype)


def partner(index, offset, count):
    if count & (count - 1) == 0:
        return index ^ offset
    return (index + count - offset) % count


def dequantized(codes_ref, scales_ref):
    rows, groups = codes_ref.shape[0], scales_ref.shape[0]
    each = rows // groups
    parts = [
        codes_ref[g * each : (g + 1) * each, :].astype(F32) * scales_ref[g : g + 1, :]
        for g in range(groups)
    ]
    return parts[0] if groups == 1 else jnp.concatenate(parts, axis=0)


def husband_kernel(codes_ref, scales_ref, out_ref):
    out_ref[...] = jnp.transpose(dequantized(codes_ref, scales_ref)).astype(BF16)


def wife_kernel(codes_ref, scales_ref, out_ref):
    out_ref[...] = dequantized(codes_ref, scales_ref).astype(BF16)


def halves(values):
    high = values.astype(BF16).astype(F32)
    return high, (values - high).astype(BF16).astype(F32)


def two_rows(values):
    high, low = halves(values)
    row = lax.broadcasted_iota(jnp.int32, (8, values.shape[1]), 0)
    return jnp.where(row == 0, high, jnp.where(row == 1, low, 0.0)).astype(BF16)


def tile_kernel(wives, traits_ref, affinity_ref, *refs):
    wife_refs, (tile_ref, sums_ref) = refs[:wives], refs[wives:]
    left = lax.dot_general(
        affinity_ref[...], traits_ref[...], (((0,), (0,)), ((), ())), preferred_element_type=F32
    ).astype(BF16)
    total = None
    at = 0
    for wife_ref in wife_refs:
        rows = wife_ref.shape[0]
        step = 256 if rows % 256 == 0 else rows
        for start in range(0, rows, step):
            scores = jnp.dot(wife_ref[start : start + step, :], left, preferred_element_type=F32)
            values = jnp.exp(scores)
            tile_ref[at : at + step, :] = values.astype(BF16)
            part = values.reshape(step // 8, 8, values.shape[1]).sum(axis=0)
            total = part if total is None else total + part
            at += step
    sums_ref[...] = total.sum(axis=0, keepdims=True)


class Layout:
    def __init__(self, chips, inner, wif, blk, pieces, width):
        self.chips, self.inner, self.wif, self.blk = chips, inner, wif, blk
        self.pieces, self.width = pieces, width
        self.outer = chips // pieces

    def places(self):
        hh, wif = lax.axis_index("hh"), lax.axis_index("wif")
        outer_at = hh // self.inner
        inner_at = (hh % self.inner) * self.wif + wif
        return [
            partner(outer_at, a, self.outer) * self.pieces + partner(inner_at, b, self.pieces)
            for b in range(self.pieces)
            for a in range(self.outer)
        ]

    def local_row(self, table_ref, b):
        places = self.places()
        rows = [
            table_ref[pl.ds(places[b * self.outer + a], 1), :] for a in range(self.outer)
        ]
        return rows[0] if len(rows) == 1 else jnp.concatenate(rows, axis=1)

    def store_row(self, table_ref, b, row):
        places = self.places()
        for a in range(self.outer):
            table_ref[pl.ds(places[b * self.outer + a], 1), :] = row[:, a * self.blk : (a + 1) * self.blk]


def pack_kernel(lay, mass_ref, *refs):
    sums, (out_ref, table_ref) = refs[: lay.pieces], refs[lay.pieces :]
    for b in range(lay.pieces):
        lay.store_row(table_ref, b, sums[b][...])
    table = table_ref[...]
    mass = mass_ref[...]
    for g in range(lay.chips):
        out_ref[g, : lay.chips, :] = table
        out_ref[g, lay.chips : lay.chips + lay.wif, :] = mass


def column_sums(lay, table_ref, tiles):
    total = None
    for b in range(lay.pieces):
        part = lax.dot_general(
            two_rows(lay.local_row(table_ref, b)),
            tiles[b][...],
            (((1,), (1,)), ((), ())),
            preferred_element_type=F32,
        )
        total = part if total is None else total + part
    return total[0:1, :] + total[1:2, :]


def first_rows_kernel(lay, count_w, got_ref, *refs):
    tiles, (cols_ref, mass_ref, table_ref) = refs[: lay.pieces], refs[lay.pieces :]
    sums = got_ref[:, : lay.chips, :].sum(axis=0)
    for g in range(lay.chips):
        mass_ref[g : g + 1, :] = got_ref[g, lay.chips + g % lay.wif : lay.chips + g % lay.wif + 1, :]
    table_ref[...] = mass_ref[...] / (sums / count_w)
    cols_ref[...] = column_sums(lay, table_ref, tiles)


def later_rows_kernel(lay, count_w, got_ref, mass_ref, *refs):
    tiles, (cols_ref, table_ref, own_ref) = refs[: lay.pieces], refs[lay.pieces :]
    table_ref[...] = mass_ref[...] / (got_ref[...].sum(axis=0) / count_w)
    cols_ref[...] = column_sums(lay, table_ref, tiles)
    start = lax.axis_index("hh") * lay.wif
    for y in range(lay.wif):
        own_ref[y : y + 1, :] = table_ref[pl.ds(start + y, 1), :]


def column_potential(count_h, shift, mine_ref, theirs_ref, mass_ref):
    theirs = theirs_ref[...]
    if shift:
        theirs = jnp.concatenate([theirs[:, shift:], theirs[:, :shift]], axis=1)
        total = mine_ref[...] + theirs
    else:
        total = mine_ref[...]
    return mass_ref[...] / (total / count_h)


def columns_kernel(lay, count_h, shift, mine_ref, theirs_ref, mass_ref, *refs):
    tiles, (out_ref, table_ref) = refs[: lay.pieces], refs[lay.pieces :]
    columns = two_rows(column_potential(count_h, shift, mine_ref, theirs_ref, mass_ref))
    for b in range(lay.pieces):
        sums = jnp.dot(columns, tiles[b][...], preferred_element_type=F32)
        lay.store_row(table_ref, b, sums[0:1, :] + sums[1:2, :])
    table = table_ref[...]
    for g in range(lay.chips):
        out_ref[g] = table


def projected_kernel(lay, table_ref, *refs):
    traits, tiles = refs[: lay.pieces], refs[lay.pieces : 2 * lay.pieces]
    out_ref = refs[2 * lay.pieces]
    total = None
    for b in range(lay.pieces):
        high, low = halves(traits[b][...].astype(F32) * lay.local_row(table_ref, b))
        for half in (high, low):
            part = lax.dot_general(
                half.astype(BF16), tiles[b][...], (((1,), (1,)), ((), ())), preferred_element_type=F32
            )
            total = part if total is None else total + part
    out_ref[...] = total


def moments_of(scale, columns, projected_ref, wife_refs):
    high, low = halves(projected_ref[...] * columns)
    total = None
    at = 0
    for wife_ref in wife_refs:
        rows = wife_ref.shape[0]
        for half in (high, low):
            part = jnp.dot(half[:, at : at + rows].astype(BF16), wife_ref[...], preferred_element_type=F32)
            total = part if total is None else total + part
        at += rows
    return total * scale


def moments_kernel(count_h, shift, scale, wives, devices, mine_ref, theirs_ref, mass_ref, projected_ref, *refs):
    wife_refs, (out_ref, first_ref, last_ref) = refs[:wives], refs[wives:]
    columns = column_potential(count_h, shift, mine_ref, theirs_ref, mass_ref)
    square = moments_of(scale, columns, projected_ref, wife_refs)
    traits = square.shape[0]
    first_ref[...] = square[:, :128]
    last_ref[:, : traits - 128] = square[:, 128:]
    even, odd = pl.ds(0, traits // 2, stride=2), pl.ds(1, traits // 2, stride=2)
    odd_first = first_ref[odd, :]
    thirds = (
        first_ref[even, :],
        jnp.concatenate([last_ref[even, :][:, : traits - 128], odd_first[:, : 256 - traits]], axis=1),
        jnp.concatenate([odd_first[:, 256 - traits :], last_ref[odd, :][:, : traits - 128]], axis=1),
    )
    each = traits // 2 // devices
    own = wife_refs[0].shape[0] // 128
    for d in range(devices):
        for q in range(3):
            out_ref[d, q * each : (q + 1) * each, :] = thirds[q][d * each : (d + 1) * each, :]
        for k in range(own):
            out_ref[d, 3 * each + k : 3 * each + k + 1, :] = columns[:, k * 128 : (k + 1) * 128]


def finish_kernel(wif, each, own, got_ref, cols_ref, moments_ref):
    devices = got_ref.shape[0]
    total = got_ref[:, : 3 * each, :].sum(axis=0)
    for q in range(3):
        for k in range(each):
            moments_ref[3 * k + q : 3 * k + q + 1, :] = total[q * each + k : q * each + k + 1, :]
    y = lax.axis_index("wif")
    for h in range(devices // wif):
        cols_ref[h * own : (h + 1) * own, :] = got_ref[h * wif + y, 3 * each : 3 * each + own, :]


def plain_moments_kernel(
    count_h, shift, scale, wives, mine_ref, theirs_ref, mass_ref, projected_ref, *refs
):
    wife_refs, (cols_ref, out_ref) = refs[:wives], refs[wives:]
    columns = column_potential(count_h, shift, mine_ref, theirs_ref, mass_ref)
    out_ref[...] = moments_of(scale, columns, projected_ref, wife_refs)
    cols_ref[...] = columns[:, : cols_ref.shape[1]]


def solution(mesh):
    hus, wif = mesh.shape["hus"], mesh.shape["wif"]
    cores = 2 if hus % 2 == 0 else 1
    hh = hus // cores
    fine = Mesh(mesh.devices.reshape(hh, cores, wif), AXES)
    inner = 2 if hh % 2 == 0 else 1
    outer = hh // inner
    chips, pieces, devices = hh * wif, inner * wif, hus * wif

    def flat(o, i, c):
        h, y = o * inner + i // wif, i % wif
        return (h * cores + c) * wif + y

    members = [(o, i, c) for o in range(outer) for i in range(pieces) for c in range(cores)]

    def from_outer(value, step):
        pairs = [(flat(partner(o, step, outer), i, c), flat(o, i, c)) for o, i, c in members]
        return lax.ppermute(value, AXES, pairs)

    def from_inner(value, step):
        pairs = [(flat(o, partner(i, step, pieces), c), flat(o, i, c)) for o, i, c in members]
        return lax.ppermute(value, AXES, pairs)

    def from_core(value):
        if cores == 1:
            return value
        return lax.ppermute(value, AXES, [(flat(o, i, 1 - c), flat(o, i, c)) for o, i, c in members])

    def body(husband_codes, husband_scales, wife_codes, wife_scales, affinity, husband_mass, wife_mass):
        blk, traits = husband_codes.shape
        own = wife_codes.shape[0]
        columns = own * cores
        width = outer * blk
        rows = chips * blk
        count_h, count_w = rows * cores, wife_mass.shape[0]
        lay = Layout(chips, inner, wif, blk, pieces, width)
        shift = own if cores == 2 else 0
        scale = traits / (count_h * count_w)

        (mine,) = call(husband_kernel, [shape((traits, blk), BF16)], husband_codes, husband_scales, name="husbands")
        blocks = [mine] + [from_outer(mine, step) for step in range(1, outer)]
        (own_wives,) = call(wife_kernel, [shape((own, traits), BF16)], wife_codes, wife_scales, name="wives")
        wives = [own_wives] + ([from_core(own_wives)] if cores == 2 else [])
        piece = jnp.concatenate(blocks, axis=1)
        trait_pieces = [piece] + [from_inner(piece, step) for step in range(1, pieces)]

        at = (lax.axis_index("wif") * hh + lax.axis_index("hh")) * columns
        chip_mass = lax.dynamic_slice_in_dim(wife_mass, at, columns)
        chip_mass = jnp.roll(chip_mass, -lax.axis_index("core") * own).reshape(1, columns)
        mass_rows = husband_mass.reshape(wif, blk)

        tiles, sums = [], []
        for b in range(pieces):
            tile, part = call(
                functools.partial(tile_kernel, cores),
                [shape((columns, width), BF16), shape((1, width))],
                trait_pieces[b],
                affinity,
                *wives,
                flops=2 * columns * width * traits,
                name="tile",
            )
            tiles.append(tile)
            sums.append(part)

        padded = -(-(chips + wif) // 8) * 8
        (packed,) = call(
            functools.partial(pack_kernel, lay),
            [shape((chips, padded, blk))],
            mass_rows,
            *sums,
            scratch=[pltpu.VMEM((chips, blk), F32)],
            name="pack",
        )
        got = lax.all_to_all(packed, CHIPS, 0, 0, tiled=True)
        cols, mass_table = call(
            functools.partial(first_rows_kernel, lay, count_w),
            [shape((1, columns)), shape((chips, blk))],
            got,
            *tiles,
            scratch=[pltpu.VMEM((chips, blk), F32)],
            flops=16 * rows * columns,
            name="rows",
        )
        for sweep in range(1, SWEEPS):
            theirs = from_core(cols)
            (packed,) = call(
                functools.partial(columns_kernel, lay, count_h, shift),
                [shape((chips, chips, blk))],
                cols,
                theirs,
                chip_mass,
                *tiles,
                scratch=[pltpu.VMEM((chips, blk), F32)],
                flops=16 * rows * columns,
                name="columns",
            )
            got = lax.all_to_all(packed, CHIPS, 0, 0, tiled=True)
            cols, table, row_pot = call(
                functools.partial(later_rows_kernel, lay, count_w),
                [shape((1, columns)), shape((chips, blk)), shape((wif, blk))],
                got,
                mass_table,
                *tiles,
                flops=16 * rows * columns,
                name="rows",
            )
        theirs = from_core(cols)
        (projected,) = call(
            functools.partial(projected_kernel, lay),
            [shape((traits, columns))],
            table,
            *trait_pieces,
            *tiles,
            flops=4 * rows * columns * traits,
            name="project",
        )
        row_pot = row_pot.reshape(-1)

        if 2 * traits == 3 * 128 and traits % (2 * devices) == 0 and own % 128 == 0:
            each, own_rows = traits // 2 // devices, own // 128
            used = -(-(3 * each + own_rows) // 8) * 8
            (packed,) = call(
                functools.partial(moments_kernel, count_h, shift, scale, cores, devices),
                [shape((devices, used, 128))],
                cols,
                theirs,
                chip_mass,
                projected,
                *wives,
                scratch=[pltpu.VMEM((traits, 128), F32)] * 2,
                flops=4 * traits * traits * columns,
                name="moments",
            )
            got = lax.all_to_all(packed, AXES, 0, 0, tiled=True)
            column_pot, moments = call(
                functools.partial(finish_kernel, wif, each, own_rows),
                [shape((hus * own_rows, 128)), shape((3 * each, 128))],
                got,
                name="finish",
            )
            return row_pot, column_pot.reshape(-1), moments.reshape(-1)

        own_cols, square = call(
            functools.partial(plain_moments_kernel, count_h, shift, scale, cores),
            [shape((1, own)), shape((traits, traits))],
            cols,
            theirs,
            chip_mass,
            projected,
            *wives,
            flops=4 * traits * traits * columns,
            name="moments",
        )
        column_pot = lax.all_gather(own_cols.reshape(-1), ("hh", "core"), axis=0, tiled=True)
        got = lax.all_to_all(square.reshape(devices, -1), AXES, 0, 0, tiled=True)
        return row_pot, column_pot, got.sum(axis=0)

    both = ("hh", "core", "wif")
    return jax.shard_map(
        body,
        mesh=fine,
        in_specs=(
            P(both, None),
            P(both, None),
            P(("wif", "hh", "core"), None),
            P(("wif", "hh", "core"), None),
            P(),
            P(("hh", "core")),
            P(),
        ),
        out_specs=(P(("hh", "core")), P("wif"), P(both)),
        check_vma=False,
    )
```

```python
import functools
import math

import jax
import jax.numpy as jnp
from jax import lax
from jax.experimental import pallas as pl
from jax.experimental.pallas import tpu as pltpu
from jax.sharding import Mesh
from jax.sharding import PartitionSpec as P

SWEEPS = 2
AXES = ("hh", "core", "wif")
CHIPS = ("hh", "wif")
F32 = jnp.float32
BF16 = jnp.bfloat16
VMEM = pl.BlockSpec(memory_space=pltpu.VMEM)
HBM = pl.BlockSpec(memory_space=pltpu.HBM)


def call(kernel, outs, *args, scratch=(), flops=0, limit=24 << 20, far=()):
    size = sum(a.size * a.dtype.itemsize for a in args)
    size += sum(o.size * o.dtype.itemsize for o in outs)
    return pl.pallas_call(
        kernel,
        out_shape=outs,
        in_specs=[HBM if k in far else VMEM for k in range(len(args))],
        out_specs=[VMEM] * len(outs),
        scratch_shapes=scratch,
        compiler_params=pltpu.CompilerParams(vmem_limit_bytes=limit),
        cost_estimate=pl.CostEstimate(flops=flops, bytes_accessed=size, transcendentals=0),
    )(*args)


def shape(dims, dtype=F32):
    return jax.ShapeDtypeStruct(dims, dtype)


def partner(index, offset, count):
    if count & (count - 1) == 0:
        return index ^ offset
    return (index + count - offset) % count


def widened(scales_ref, persons):
    scales = jnp.transpose(scales_ref[...])
    traits, groups = scales.shape
    each = persons // groups
    wide = [jnp.broadcast_to(scales[:, g : g + 1], (traits, each)) for g in range(groups)]
    return wide[0] if groups == 1 else jnp.concatenate(wide, axis=1)


def scales_kernel(scales_ref, out_ref):
    out_ref[...] = widened(scales_ref, out_ref.shape[1])


def husband_kernel(codes_ref, scales_ref, out_ref):
    out_ref[...] = (codes_ref[...].astype(F32) * scales_ref[...]).astype(BF16)


def wife_kernel(codes_ref, scales_ref, mass_ref, after_ref, out_ref, mass_out_ref):
    del after_ref
    values = codes_ref[...].astype(F32) * widened(scales_ref, codes_ref.shape[1])
    out_ref[...] = jnp.transpose(values).astype(BF16)
    mass_out_ref[...] = mass_ref[...]


def side_by_side(refs):
    return refs[0][...] if len(refs) == 1 else jnp.concatenate([ref[...] for ref in refs], axis=1)


def halves(values):
    high = values.astype(BF16).astype(F32)
    return high, (values - high).astype(BF16).astype(F32)


def two_rows(values):
    high, low = halves(values)
    row = lax.broadcasted_iota(jnp.int32, (8, values.shape[1]), 0)
    return jnp.where(row == 0, high, jnp.where(row == 1, low, 0.0)).astype(BF16)


def fill_tile(trait_refs, affinity_ref, wife_refs, tile_ref):
    left = lax.dot_general(
        affinity_ref[...], side_by_side(trait_refs), (((0,), (0,)), ((), ())), preferred_element_type=F32
    ).astype(BF16)
    total = None
    at = 0
    for wife_ref in wife_refs:
        rows = wife_ref.shape[0]
        step = 256 if rows % 256 == 0 else rows
        for start in range(0, rows, step):
            scores = jnp.dot(wife_ref[start : start + step, :], left, preferred_element_type=F32)
            values = jnp.exp(scores)
            tile_ref[at : at + step, :] = values.astype(BF16)
            part = values.reshape(step // 8, 8, values.shape[1]).sum(axis=0)
            total = part if total is None else total + part
            at += step
    return total.sum(axis=0, keepdims=True)


def tile_kernel(wives, affinity_ref, *refs):
    wife_refs, trait_refs, (tile_ref, sums_ref) = refs[:wives], refs[wives:-2], refs[-2:]
    sums_ref[...] = fill_tile(trait_refs, affinity_ref, wife_refs, tile_ref)


def last_tile_kernel(lay, wives, affinity_ref, mass_ref, *refs):
    wife_refs, sums = refs[:wives], refs[wives : wives + lay.pieces - 1]
    trait_refs, (tile_ref, out_ref, table_ref) = refs[wives + lay.pieces - 1 : -3], refs[-3:]
    for b in range(lay.pieces - 1):
        lay.store_row(table_ref, b, sums[b][...])
    lay.store_row(table_ref, lay.pieces - 1, fill_tile(trait_refs, affinity_ref, wife_refs, tile_ref))
    lay.spread(out_ref, 0, table_ref, lay.chips)
    lay.spread(out_ref, lay.chips * lay.blk, mass_ref, lay.wif)


class Layout:
    def __init__(self, hh, inner, cores, wif, blk, own):
        self.hh, self.inner, self.cores, self.wif, self.blk, self.own = hh, inner, cores, wif, blk, own
        self.chips, self.pieces, self.outer = hh * wif, inner * wif, hh // inner

    def places(self):
        hh, wif = lax.axis_index("hh"), lax.axis_index("wif")
        outer_at = hh // self.inner
        inner_at = (hh % self.inner) * self.wif + wif
        return [
            partner(outer_at, a, self.outer) * self.pieces + partner(inner_at, b, self.pieces)
            for b in range(self.pieces)
            for a in range(self.outer)
        ]

    def local_row(self, table_ref, b):
        places = self.places()
        rows = [
            table_ref[pl.ds(places[b * self.outer + a], 1), :] for a in range(self.outer)
        ]
        return rows[0] if len(rows) == 1 else jnp.concatenate(rows, axis=1)

    def spread(self, out_ref, start, table_ref, count):
        for k in range(count):
            row = jnp.broadcast_to(table_ref[k : k + 1, :], (out_ref.shape[0], self.blk))
            out_ref[:, start + k * self.blk : start + (k + 1) * self.blk] = row

    def summed(self, table_ref, got_ref):
        total = got_ref[:, : self.chips * self.blk].sum(axis=0, keepdims=True)
        for g in range(self.chips):
            table_ref[g : g + 1, :] = total[:, g * self.blk : (g + 1) * self.blk]

    def store_row(self, table_ref, b, row):
        places = self.places()
        for a in range(self.outer):
            table_ref[pl.ds(places[b * self.outer + a], 1), :] = row[:, a * self.blk : (a + 1) * self.blk]


def column_sums(lay, table_ref, tiles):
    total = None
    for b in range(lay.pieces):
        part = lax.dot_general(
            two_rows(lay.local_row(table_ref, b)),
            tiles[b][...],
            (((1,), (1,)), ((), ())),
            preferred_element_type=F32,
        )
        total = part if total is None else total + part
    return total[0:1, :] + total[1:2, :]


def first_rows_kernel(lay, count_w, got_ref, *refs):
    tiles, (cols_ref, mass_ref, table_ref) = refs[: lay.pieces], refs[lay.pieces :]
    lay.summed(table_ref, got_ref)
    for g in range(lay.chips):
        start = (lay.chips + g % lay.wif) * lay.blk
        mass_ref[g : g + 1, :] = got_ref[g : g + 1, start : start + lay.blk]
    table_ref[...] = mass_ref[...] / (table_ref[...] / count_w)
    cols_ref[...] = column_sums(lay, table_ref, tiles)


def later_rows_kernel(lay, count_w, got_ref, mass_ref, *refs):
    tiles, (cols_ref, table_ref) = refs[: lay.pieces], refs[lay.pieces :]
    table_ref[...] = mass_ref[...] / (got_ref[...].sum(axis=0) / count_w)
    cols_ref[...] = column_sums(lay, table_ref, tiles)


def column_potential(lay, count_h, mine_ref, theirs_ref, mass_ref):
    total = mine_ref[...]
    core = lax.axis_index("core")
    first = ((lax.axis_index("wif") * lay.hh + lax.axis_index("hh")) * lay.cores) * lay.own
    starts = [first + core * lay.own]
    if lay.cores == 2:
        theirs = theirs_ref[...]
        total = total + jnp.concatenate([theirs[:, lay.own :], theirs[:, : lay.own]], axis=1)
        starts.append(first + (1 - core) * lay.own)
    lanes = mass_ref.shape[1]
    mass = [
        mass_ref[pl.ds(start // lanes + k, 1), :] for start in starts for k in range(lay.own // lanes)
    ]
    mass = mass[0] if len(mass) == 1 else jnp.concatenate(mass, axis=1)
    return mass / (total / count_h)


def spread_table(out_ref, table_ref):
    table = table_ref[...]
    for g in range(out_ref.shape[0]):
        out_ref[g] = table


def columns_kernel(lay, count_h, mine_ref, theirs_ref, mass_ref, *refs):
    tiles, (out_ref, table_ref) = refs[: lay.pieces], refs[lay.pieces :]
    columns = two_rows(column_potential(lay, count_h, mine_ref, theirs_ref, mass_ref))
    for b in range(lay.pieces):
        sums = jnp.dot(columns, tiles[b][...], preferred_element_type=F32)
        lay.store_row(table_ref, b, sums[0:1, :] + sums[1:2, :])
    spread_table(out_ref, table_ref)


def projected_kernel(lay, counts, table_ref, *refs):
    out_ref, tiles, at = refs[-1], refs[-1 - lay.pieces : -1], 0
    total = None
    for b in range(lay.pieces):
        traits = side_by_side(refs[at : at + counts[b]])
        at += counts[b]
        high, low = halves(traits.astype(F32) * lay.local_row(table_ref, b))
        part = lax.dot_general(
            jnp.concatenate([high, low], axis=0).astype(BF16),
            tiles[b][...],
            (((1,), (1,)), ((), ())),
            preferred_element_type=F32,
        )
        total = part if total is None else total + part
    half = total.shape[0] // 2
    total = total[:half, :] + total[half:, :]
    out_ref[...] = total


def moments_of(scale, columns, projected_ref, wife_refs):
    high, low = halves(projected_ref[...] * columns)
    total = None
    at = 0
    for wife_ref in wife_refs:
        rows = wife_ref.shape[0]
        for half in (high, low):
            part = jnp.dot(half[:, at : at + rows].astype(BF16), wife_ref[...], preferred_element_type=F32)
            total = part if total is None else total + part
        at += rows
    return total * scale


def moments_kernel(lay, count_h, scale, wives, devices, mine_ref, theirs_ref, mass_ref, projected_ref, *refs):
    wife_refs, (out_ref, first_ref, last_ref, third_ref) = refs[:wives], refs[wives:]
    columns = column_potential(lay, count_h, mine_ref, theirs_ref, mass_ref)
    square = moments_of(scale, columns, projected_ref, wife_refs)
    traits = square.shape[0]
    first_ref[...] = square[:, :128]
    last_ref[:, : traits - 128] = square[:, 128:]
    even, odd = pl.ds(0, traits // 2, stride=2), pl.ds(1, traits // 2, stride=2)
    odd_first = first_ref[odd, :]
    thirds = (
        first_ref[even, :],
        jnp.concatenate([last_ref[even, :][:, : traits - 128], odd_first[:, : 256 - traits]], axis=1),
        jnp.concatenate([odd_first[:, 256 - traits :], last_ref[odd, :][:, : traits - 128]], axis=1),
    )
    each = traits // 2 // devices
    for q in range(3):
        third_ref[q * traits // 2 : (q + 1) * traits // 2, :] = thirds[q]
    for k in range(each):
        for q in range(3):
            at = 3 * k + q
            rows = third_ref[pl.ds(q * traits // 2 + k, devices, stride=each), :]
            out_ref[:, at * 128 : (at + 1) * 128] = rows
    start = 3 * each * 128
    out_ref[:, start:] = jnp.broadcast_to(columns[:, : lay.own], (devices, lay.own))


def finish_kernel(lay, each, got_ref, table_ref, cols_ref, moments_ref, rows_ref):
    size = 3 * each * 128
    total = got_ref[:, :size].sum(axis=0, keepdims=True)
    for k in range(3 * each):
        moments_ref[k : k + 1, :] = total[:, k * 128 : (k + 1) * 128]
    y = lax.axis_index("wif")
    own = lay.own // 128
    for h in range(got_ref.shape[0] // lay.wif):
        row = got_ref[pl.ds(h * lay.wif + y, 1), size:]
        for k in range(own):
            cols_ref[h * own + k : h * own + k + 1, :] = row[:, k * 128 : (k + 1) * 128]
    start = lax.axis_index("hh") * lay.wif
    for k in range(lay.wif):
        rows_ref[k : k + 1, :] = table_ref[pl.ds(start + k, 1), :]


def plain_moments_kernel(
    lay, count_h, scale, wives, mine_ref, theirs_ref, mass_ref, projected_ref, *refs
):
    wife_refs, (cols_ref, out_ref) = refs[:wives], refs[wives:]
    columns = column_potential(lay, count_h, mine_ref, theirs_ref, mass_ref)
    out_ref[...] = moments_of(scale, columns, projected_ref, wife_refs)
    cols_ref[...] = columns[:, : cols_ref.shape[1]]


def solution(mesh):
    hus, wif = mesh.shape["hus"], mesh.shape["wif"]
    cores = 2 if hus % 2 == 0 else 1
    hh = hus // cores
    fine = Mesh(mesh.devices.reshape(hh, cores, wif), AXES)
    inner = 2 if hh % 2 == 0 else 1
    outer = hh // inner
    chips, pieces, devices = hh * wif, inner * wif, hus * wif

    def flat(o, i, c):
        h, y = o * inner + i // wif, i % wif
        return (h * cores + c) * wif + y

    members = [(o, i, c) for o in range(outer) for i in range(pieces) for c in range(cores)]

    def from_outer(value, step):
        pairs = [(flat(partner(o, step, outer), i, c), flat(o, i, c)) for o, i, c in members]
        return lax.ppermute(value, AXES, pairs)

    def from_inner(value, step):
        pairs = [(flat(o, partner(i, step, pieces), c), flat(o, i, c)) for o, i, c in members]
        return lax.ppermute(value, AXES, pairs)

    def from_core(value):
        if cores == 1:
            return value
        return lax.ppermute(value, AXES, [(flat(o, i, 1 - c), flat(o, i, c)) for o, i, c in members])

    def body(husband_codes, husband_scales, wife_codes, wife_scales, affinity, husband_mass, wife_mass):
        blk, traits = husband_codes.shape
        own = wife_codes.shape[0]
        columns = own * cores
        width = outer * blk
        rows = chips * blk
        count_h, count_w = rows * cores, wife_mass.shape[0]
        lay = Layout(hh, inner, cores, wif, blk, own)
        scale = traits / (count_h * count_w)

        (scales,) = call(scales_kernel, [shape((traits, blk))], husband_scales)
        (mine,) = call(husband_kernel, [shape((traits, blk), BF16)], husband_codes.T, scales)
        blocks = [mine] + [from_outer(mine, step) for step in range(1, outer)]
        piece = blocks[0] if outer == 1 else jnp.concatenate(blocks, axis=1)
        mass_rows = husband_mass.reshape(wif, blk)
        trait_pieces = [[piece]] + [[from_inner(piece, step)] for step in range(1, pieces)]
        own_wives, mass_rows = call(
            wife_kernel,
            [shape((own, traits), BF16), shape((wif, blk))],
            wife_codes.T,
            wife_scales,
            mass_rows,
            piece,
            far=(3,),
        )
        wives = [own_wives] + ([from_core(own_wives)] if cores == 2 else [])
        counts = [len(piece) for piece in trait_pieces]

        lanes = math.gcd(own, 128)
        wife_rows = wife_mass.reshape(-1, lanes)

        tiles, sums = [], []
        for b in range(pieces - 1):
            tile, part = call(
                functools.partial(tile_kernel, cores),
                [shape((columns, width), BF16), shape((1, width))],
                affinity,
                *wives,
                *trait_pieces[b],
                flops=2 * columns * width * traits,
            )
            tiles.append(tile)
            sums.append(part)
        tile, packed = call(
            functools.partial(last_tile_kernel, lay, cores),
            [shape((columns, width), BF16), shape((chips, (chips + wif) * blk))],
            affinity,
            mass_rows,
            *wives,
            *sums,
            *trait_pieces[-1],
            scratch=[pltpu.VMEM((chips, blk), F32)],
            flops=2 * columns * width * traits,
        )
        tiles.append(tile)
        got = lax.all_to_all(packed, CHIPS, 0, 0, tiled=True)
        cols, mass_table = call(
            functools.partial(first_rows_kernel, lay, count_w),
            [shape((1, columns)), shape((chips, blk))],
            got,
            *tiles,
            scratch=[pltpu.VMEM((chips, blk), F32)],
            flops=16 * rows * columns,
        )
        for _ in range(1, SWEEPS):
            theirs = from_core(cols)
            (packed,) = call(
                functools.partial(columns_kernel, lay, count_h),
                [shape((chips, chips, blk))],
                cols,
                theirs,
                wife_rows,
                *tiles,
                scratch=[pltpu.VMEM((chips, blk), F32)],
                flops=16 * rows * columns,
            )
            got = lax.all_to_all(packed, CHIPS, 0, 0, tiled=True)
            cols, table = call(
                functools.partial(later_rows_kernel, lay, count_w),
                [shape((1, columns)), shape((chips, blk))],
                got,
                mass_table,
                *tiles,
                flops=16 * rows * columns,
            )
        theirs = from_core(cols)
        (projected,) = call(
            functools.partial(projected_kernel, lay, counts),
            [shape((traits, columns))],
            table,
            *[block for piece in trait_pieces for block in piece],
            *tiles,
            flops=4 * rows * columns * traits,
        )
        if 2 * traits == 3 * 128 and traits % (2 * devices) == 0 and own % 128 == 0:
            each = traits // 2 // devices
            (packed,) = call(
                functools.partial(moments_kernel, lay, count_h, scale, cores, devices),
                [shape((devices, 3 * each * 128 + own))],
                cols,
                theirs,
                wife_rows,
                projected,
                *wives,
                scratch=[pltpu.VMEM((traits, 128), F32)] * 2 + [pltpu.VMEM((3 * traits // 2, 128), F32)],
                flops=4 * traits * traits * columns,
            )
            got = lax.all_to_all(packed, AXES, 0, 0, tiled=True)
            column_pot, moments, row_pot = call(
                functools.partial(finish_kernel, lay, each),
                [shape((hus * own // 128, 128)), shape((3 * each, 128)), shape((wif, blk))],
                got,
                table,
            )
            return row_pot.reshape(-1), column_pot.reshape(-1), moments.reshape(-1)

        own_cols, square = call(
            functools.partial(plain_moments_kernel, lay, count_h, scale, cores),
            [shape((1, own)), shape((traits, traits))],
            cols,
            theirs,
            wife_rows,
            projected,
            *wives,
            flops=4 * traits * traits * columns,
        )
        column_pot = lax.all_gather(own_cols.reshape(-1), ("hh", "core"), axis=0, tiled=True)
        got = lax.all_to_all(square.reshape(devices, -1), AXES, 0, 0, tiled=True)
        start = lax.axis_index("hh") * wif
        row_pot = lax.dynamic_slice_in_dim(table, start, wif).reshape(-1)
        return row_pot, column_pot, got.sum(axis=0)

    both = ("hh", "core", "wif")
    return jax.shard_map(
        body,
        mesh=fine,
        in_specs=(
            P(both, None),
            P(both, None),
            P(("wif", "hh", "core"), None),
            P(("wif", "hh", "core"), None),
            P(),
            P(("hh", "core")),
            P(),
        ),
        out_specs=(P(("hh", "core")), P("wif"), P(both)),
        check_vma=False,
    )
```
